32 devices in a mesh: groups: 2 (over x), node: 8 (over z, y), rep: 2 (over core).
Axes of the slice: x: 2, y: 2, z: 4, core: 2. Of those that a mesh axis runs over, the one named last changes fastest.
Arguments:
- normed_input: bfloat16 [4, 1024, 5120], P(('groups', 'rep'), 'node'), parts along dimension 0, may hold values from -6 to 6
- queries: bfloat16 [4, 1024, 2560], P(('groups', 'rep'), 'node'), parts along dimension 0, may hold values from -120 to 120
- rotated_key_heads: bfloat16 [4, 1024, 512], P(('groups', 'rep'), 'node'), parts along dimension 0, may hold values from -6 to 6
- frozen_value_rows: bfloat16 [4, 1024, 512], P(('groups', 'rep'), 'node'), parts along dimension 0, may hold values from -6 to 6
- adapter_down_weight: bfloat16 [5120, 32], replicated, may hold values from -0.078125 to 0.078125
- adapter_up_weight: bfloat16 [32, 512], replicated, may hold values from -1 to 1
- output_gradient: bfloat16 [4, 1024, 2560], P(('groups', 'rep'), 'node'), parts along dimension 0, may hold values from -6 to 6
- parents: int32 [4, 8], P(('groups', 'rep')), parts along dimension 0, may hold values from -1 to 6, as said below
- lengths: int32 [4, 8], P(('groups', 'rep')), parts along dimension 0, may hold values from 32 to 128, as said below
Outputs:
- attended: bfloat16 [4, 1024, 2560], P(('groups', 'rep'), 'node'), parts along dimension 0
- query_grad: bfloat16 [4, 1024, 2560], P(('groups', 'rep'), 'node'), parts along dimension 0
- down_grad: float32 [10240, 32], P('groups'), parts along dimension 0
- up_grad: float32 [64, 512], P('groups'), parts along dimension 0
The draws below stay inside these ranges and needn't reach their ends.
There are 2 independent parts, one for each index of `groups`. The reference program is written for one: setup_inputs(seed, part) draws one part's arguments, and reference() takes and returns one part's arrays. A program takes and returns all parts, laid end to end along the dimension named above; an argument that names none is the same for every part. Nothing has to cross between parts.
Inputs may be any that keep to these rules, and one draw needn't show every extreme that they name: `parents`: slots 0 to 1 form the shared prompt, each the parent of the next, slot 0 the root. Every other slot's parent is slot 1 or a slot below it, and every ancestor of a slot s outside the prompt lies among the slots s - 5 to s - 1. `lengths`: prompt blocks are full.
All inputs are finite; a program needn't handle non-finite values.
Results may differ from the reference program's by a relative error of at most 0.0062.
Values may be sent and summed in bfloat16 or wider, within the bound.
A program may use at most 128 MiB of HBM per device.

```python
import jax
import jax.numpy as jnp
from jax import lax

MODEL_WIDTH = 5120
HQ = 20
KEY_HEADS = 4
HEAD_SIZE = 128
ADAPTER_RANK = 32
BLK = 128
PROMPT = 2
SPAN = 5
TREES = 2
ROWS = 1024
N_NODE = 8
N_REP = 2


def tree_links(tree_key):
    position_index = jnp.arange(N_NODE, dtype=jnp.int32)
    order_scores = jax.random.randint(tree_key, (N_NODE, N_NODE), 0, 1024, dtype=jnp.int32)
    start = jnp.where(position_index < PROMPT, position_index - 1, 0).astype(jnp.int32)

    def extend(carried, tree_position):
        parent_row, lowest = carried
        permitted_mask = (position_index == PROMPT - 1) | (position_index >= PROMPT) & (position_index < tree_position) & (position_index >= tree_position - SPAN) & (lowest >= tree_position - SPAN)
        extra_logit = jnp.where(position_index == tree_position - 1, 400, 0).astype(jnp.int32)
        sorted_order = jnp.where(permitted_mask, (order_scores[tree_position] + extra_logit) * 64 + position_index, -1)
        chosen = jnp.argmax(sorted_order).astype(jnp.int32)
        parent_row = parent_row.at[tree_position].set(chosen)
        lowest = lowest.at[tree_position].set(jnp.where(chosen == PROMPT - 1, tree_position, lowest[chosen]).astype(jnp.int32))
        return ((parent_row, lowest), None)
    (parent_row, lowest), unused = lax.scan(extend, (start, position_index), jnp.arange(PROMPT, N_NODE, dtype=jnp.int32))
    return parent_row


def draw_parents(key, part):
    tree_keys = jax.random.split(jax.random.fold_in(key, 5), N_REP)
    return jax.vmap(tree_links)(tree_keys).astype(jnp.int32)


def draw_lengths(key, part):
    drawn = jax.random.randint(jax.random.fold_in(key, 7), (N_REP, N_NODE), BLK // 4, BLK + 1, dtype=jnp.int32)
    position_index = jnp.arange(N_NODE, dtype=jnp.int32)[None, :]
    drawn = jnp.where(position_index < PROMPT, BLK, drawn)
    drawn = jnp.where(position_index == PROMPT, BLK // 4, drawn)
    return drawn.astype(jnp.int32)


def key_table(key):
    table = jnp.clip(jax.random.normal(jax.random.fold_in(key, 11), (N_REP, N_NODE * BLK, KEY_HEADS * HEAD_SIZE), jnp.float32), -5.0, 5.0)
    return table


def draw_rotated_key_heads(key, part):
    return key_table(key).astype(jnp.bfloat16)


def draw_queries(key, part):
    entries = jnp.clip(jax.random.normal(jax.random.fold_in(key, 13), (N_REP, N_NODE * BLK, HQ * HEAD_SIZE), jnp.float32), -5.0, 5.0)
    return entries.astype(jnp.bfloat16)


def steps_of(rng, extent, cuts, low, largest):
    loudness, own = 1.0, jax.random.fold_in(rng, 6)
    for dim, blocks in cuts:
        heights = jnp.exp(jax.random.uniform(jax.random.fold_in(own, dim), (blocks,), jnp.float32, low / len(cuts), largest / len(cuts)))
        loudness = loudness * jnp.repeat(heights, extent[dim] // blocks).reshape([-1 if axis == dim else 1 for axis in range(len(extent))])
    return loudness


def normal_values(rng, dims, deviation, most, pieces=(), kind=jnp.bfloat16):
    values = deviation * jax.random.normal(rng, dims, jnp.float32)
    if pieces:
        values = values * steps_of(rng, dims, pieces, -0.22, 0.18)
    return jnp.clip(values, -most, most).astype(kind)


def setup_inputs(seed: int = 0, part: int = 0) -> dict:
    key_of = jax.random.split(jax.random.key(seed), 10)
    part_splits = jax.random.split(jax.random.fold_in(key_of[9], part), 10)
    normed_input = normal_values(part_splits[0], (TREES, ROWS, MODEL_WIDTH), 1.0, 6.0, ((0, 2), (1, 8)))
    queries = draw_queries(jax.random.fold_in(jax.random.fold_in(key_of[9], part), 71), part)
    rotated_key_heads = draw_rotated_key_heads(jax.random.fold_in(jax.random.fold_in(key_of[9], part), 71), part)
    frozen_value_rows = normal_values(part_splits[3], (TREES, ROWS, KEY_HEADS * HEAD_SIZE), 1.0, 6.0, ((0, 2), (1, 8)))
    adapter_down_weight = normal_values(key_of[4], (MODEL_WIDTH, ADAPTER_RANK), MODEL_WIDTH ** -0.5, 0.078125)
    adapter_up_weight = normal_values(key_of[5], (ADAPTER_RANK, KEY_HEADS * HEAD_SIZE), ADAPTER_RANK ** -0.5, 1.0)
    output_gradient = normal_values(part_splits[6], (TREES, ROWS, HQ * HEAD_SIZE), 1.0, 6.0, ((0, 2), (1, 8)))
    parents = draw_parents(jax.random.fold_in(jax.random.fold_in(key_of[9], part), 71), part)
    lengths = draw_lengths(jax.random.fold_in(jax.random.fold_in(key_of[9], part), 71), part)
    return dict(normed_input=normed_input, queries=queries, rotated_key_heads=rotated_key_heads, frozen_value_rows=frozen_value_rows, adapter_down_weight=adapter_down_weight, adapter_up_weight=adapter_up_weight, output_gradient=output_gradient, parents=parents, lengths=lengths)


NEGATIVE = -1.0e30
HIGHEST = lax.Precision.HIGHEST


def chain_of(parent_row):
    current = parent_row
    columns = []
    for height in range(PROMPT + SPAN):
        columns.append(current)
        current = jnp.where(current >= 0, parent_row[jnp.maximum(current, 0)], -1).astype(jnp.int32)
    return jnp.stack(columns, 1)


def reference(normed_input, queries, rotated_key_heads, frozen_value_rows, adapter_down_weight, adapter_up_weight, output_gradient, parents, lengths):
    trees = normed_input.shape[0]
    slot_count = parents.shape[1]
    block_rows = normed_input.shape[1] // slot_count
    groups_per = HQ // KEY_HEADS
    key_value_width = KEY_HEADS * HEAD_SIZE
    inverse_root = HEAD_SIZE ** -0.5
    position = jnp.arange(block_rows, dtype=jnp.int32)
    adapter_inner = jnp.dot(normed_input.reshape(-1, MODEL_WIDTH), adapter_down_weight, preferred_element_type=jnp.float32).astype(jnp.bfloat16)
    value_rows = frozen_value_rows.reshape(-1, key_value_width).astype(jnp.float32) + jnp.dot(adapter_inner, adapter_up_weight, preferred_element_type=jnp.float32)
    value_rows = value_rows.astype(jnp.bfloat16).reshape(trees, slot_count, block_rows, KEY_HEADS, HEAD_SIZE)
    adapter_inner = adapter_inner.reshape(trees, slot_count * block_rows, ADAPTER_RANK)
    up_weight_float = adapter_up_weight.astype(jnp.float32)
    count = 1 + PROMPT + SPAN
    not_first = (jnp.arange(count, dtype=jnp.int32) > 0)[:, None, None]
    causal = position[None, :] <= position[:, None]
    down_total = jnp.zeros((MODEL_WIDTH, ADAPTER_RANK), jnp.float32)
    up_total = jnp.zeros((ADAPTER_RANK, key_value_width), jnp.float32)
    attended_all = []
    grads_all = []
    for tree in range(trees):
        own_ids = jnp.arange(slot_count, dtype=jnp.int32)[:, None]
        cand_ids = jnp.concatenate([own_ids, chain_of(parents[tree])], 1).astype(jnp.int32)
        safe_ids = jnp.maximum(cand_ids, 0).astype(jnp.int32)
        keys_tree = rotated_key_heads[tree].reshape(slot_count, block_rows, KEY_HEADS, HEAD_SIZE).astype(jnp.float32)
        values_tree = value_rows[tree].astype(jnp.float32)
        query_tree = queries[tree].reshape(slot_count, block_rows, KEY_HEADS, groups_per, HEAD_SIZE).astype(jnp.float32)
        grad_tree = output_gradient[tree].reshape(slot_count, block_rows, KEY_HEADS, groups_per, HEAD_SIZE)
        length_row = lengths[tree]

        def slot_work(tree_position):
            picked = safe_ids[tree_position]
            usable = cand_ids[tree_position] >= 0
            keys_here = keys_tree[picked]
            values_here = values_tree[picked]
            key_live = position[None, :] < length_row[picked][:, None]
            permitted_mask = (causal[None] | not_first) & key_live[:, None, :] & usable[:, None, None]
            logits = jnp.einsum("ikgd,cjkd->ckgij", query_tree[tree_position], keys_here, precision=HIGHEST) * inverse_root
            logits = jnp.where(permitted_mask[:, None, None], logits, NEGATIVE)
            highest = jnp.max(logits, axis=(0, 4))
            totals = jnp.sum(jnp.exp(logits - highest[None, :, :, :, None]), axis=(0, 4))
            log_total = highest + jnp.log(totals)
            weights = jnp.exp(logits - log_total[None, :, :, :, None])
            rounded = lax.optimization_barrier(weights.astype(jnp.bfloat16)).astype(jnp.float32)
            output = jnp.einsum("ckgij,cjkd->ikgd", rounded, values_here, precision=HIGHEST)
            live = position < length_row[tree_position]
            attended = jnp.where(live[:, None, None, None], output, 0.0).astype(jnp.bfloat16)
            head_gradient = jnp.where(live[:, None, None, None], grad_tree[tree_position], jnp.zeros_like(grad_tree[tree_position])).astype(jnp.float32)
            row_dots = jnp.einsum("ikgd,ikgd->kgi", head_gradient, output, precision=HIGHEST)
            pressure = jnp.einsum("ikgd,cjkd->ckgij", head_gradient, values_here, precision=HIGHEST)
            slopes = (weights * (pressure - row_dots[None, :, :, :, None]) * inverse_root).astype(jnp.bfloat16)
            slopes = lax.optimization_barrier(slopes).astype(jnp.float32)
            query_grad = jnp.einsum("ckgij,cjkd->ikgd", slopes, keys_here, precision=HIGHEST).astype(jnp.bfloat16)
            value_parts = jnp.einsum("ckgij,ikgd->cjkd", rounded, head_gradient, precision=HIGHEST)
            return attended, query_grad, value_parts

        attended, query_grad, value_parts = lax.map(slot_work, jnp.arange(slot_count, dtype=jnp.int32))
        value_total = jnp.zeros((slot_count, block_rows, KEY_HEADS, HEAD_SIZE), jnp.float32)
        value_total = value_total.at[safe_ids.reshape(-1)].add(value_parts.reshape(-1, block_rows, KEY_HEADS, HEAD_SIZE))
        value_flat = value_total.reshape(-1, key_value_width)
        projected = jnp.dot(value_flat, up_weight_float.T, precision=HIGHEST).astype(jnp.bfloat16)
        down_total = down_total + jnp.dot(normed_input[tree].T, projected, preferred_element_type=jnp.float32)
        up_total = up_total + jnp.dot(adapter_inner[tree].astype(jnp.float32).T, value_flat, precision=HIGHEST)
        attended_all.append(attended.reshape(slot_count * block_rows, HQ * HEAD_SIZE))
        grads_all.append(query_grad.reshape(slot_count * block_rows, HQ * HEAD_SIZE))
    factor = (trees * slot_count * block_rows) ** -0.5
    return jnp.stack(attended_all), jnp.stack(grads_all), down_total * factor, up_total * factor
```

```python
import functools
import math

import jax
import jax.numpy as jnp
from jax import lax
from jax.experimental import pallas as pl
from jax.experimental.pallas import tpu as pltpu
from jax.sharding import PartitionSpec as P

KEY_HEADS = 4
HEAD_SIZE = 128
PROMPT = 2
SPAN = 5
STEPS = 1 + PROMPT + SPAN
NEGATIVE = -1e30
F32 = jnp.float32
BF16 = jnp.bfloat16
NT = (((1,), (1,)), ((), ()))
NN = (((1,), (0,)), ((), ()))
TN = (((0,), (0,)), ((), ()))


def dot(a, b, dims):
    return lax.dot_general(a, b, dims, preferred_element_type=F32)


def attention_kernel(
    parents, lengths, q_ref, g_ref, k_ref, v_ref, low_ref, up_ref,
    att_ref, qg_ref, proj_ref, upg_ref,
    cand, score, out_acc, qg_acc, grad,
):
    own = lax.axis_index("node")
    head = pl.program_id(0)
    slots, block, _ = k_ref.shape
    per = q_ref.shape[1] // HEAD_SIZE
    rows = per * block
    scale = HEAD_SIZE ** -0.5

    cand[0] = own
    current = own
    count = jnp.int32(1)
    for step in range(1, STEPS):
        parent = parents[0, jnp.maximum(current, 0)]
        current = jnp.where(current >= 0, parent, -1)
        cand[step] = jnp.maximum(current, 0)
        count = count + (current >= 0).astype(jnp.int32)
    own_length = lengths[0, own]

    def stack(ref):
        return jnp.concatenate(
            [ref[:, c * HEAD_SIZE:(c + 1) * HEAD_SIZE] for c in range(per)], axis=0
        )

    live = lax.broadcasted_iota(jnp.int32, (block, HEAD_SIZE), 0) < own_length
    for c in range(per):
        part = g_ref[:, c * HEAD_SIZE:(c + 1) * HEAD_SIZE].astype(F32)
        grad[pl.ds(c * block, block), :] = jnp.where(live, part, 0.0).astype(BF16)
    query = stack(q_ref)

    column = lax.broadcasted_iota(jnp.int32, (block, block), 1)
    row = lax.broadcasted_iota(jnp.int32, (block, block), 0)

    s = dot(query, k_ref[own], NT) * (scale * math.log2(math.e))
    allowed = (column <= row) & (column < own_length)
    bias = jnp.where(allowed, 0.0, NEGATIVE)
    bias = jnp.concatenate([bias] * per, axis=0)
    s = jnp.where(bias < 0.0, NEGATIVE, s)
    score[0] = s

    def logits_step(h, top):
        slot = cand[h]
        s = dot(query, k_ref[slot], NT) * (scale * math.log2(math.e))
        col = lax.broadcasted_iota(jnp.int32, (rows, block), 1)
        s = jnp.where(col < lengths[0, slot], s, NEGATIVE)
        score[h] = s
        return jnp.maximum(top, s)

    top = lax.fori_loop(1, count, logits_step, s)
    top = jnp.max(top, axis=1, keepdims=True)

    def exp_step(h, total):
        e = jnp.exp2(score[h] - top)
        score[h] = e
        return total + e

    total = lax.fori_loop(0, count, exp_step, jnp.zeros((rows, block), F32))
    inverse = 1.0 / jnp.sum(total, axis=1, keepdims=True)

    out_acc[...] = jnp.zeros_like(out_acc)

    def output_step(h, carry):
        w = score[h] * inverse
        score[h] = w
        out_acc[...] += dot(w.astype(BF16), v_ref[cand[h]], NN)
        return carry

    lax.fori_loop(0, count, output_step, 0)

    dots = jnp.sum(grad[...].astype(F32) * out_acc[...], axis=1, keepdims=True)
    for c in range(per):
        part = out_acc[pl.ds(c * block, block), :]
        att_ref[:, c * HEAD_SIZE:(c + 1) * HEAD_SIZE] = jnp.where(live, part, 0.0).astype(BF16)

    @pl.when(head == 0)
    def _():
        proj_ref[...] = jnp.zeros_like(proj_ref)

    qg_acc[...] = jnp.zeros_like(qg_acc)
    upg_ref[...] = jnp.zeros_like(upg_ref)

    def backward_step(h, carry):
        slot = cand[h]
        g = grad[...]
        w = score[h]
        pressure = dot(g, v_ref[slot], NT)
        slopes = (w * (pressure - dots) * scale).astype(BF16)
        qg_acc[...] += dot(slopes, k_ref[slot], NN)
        value_grad = dot(w.astype(BF16), g, TN)
        high = value_grad.astype(BF16)
        lowp = (value_grad - high.astype(F32)).astype(BF16)
        proj_ref[slot] += dot(up_ref[...], high, NT) + dot(up_ref[...], lowp, NT)
        upg_ref[...] += dot(low_ref[slot], high, NN) + dot(low_ref[slot], lowp, NN)
        return carry

    lax.fori_loop(0, count, backward_step, 0)
    for c in range(per):
        qg_ref[:, c * HEAD_SIZE:(c + 1) * HEAD_SIZE] = qg_acc[pl.ds(c * block, block), :].astype(BF16)


def attention(parents, lengths, q, g, k_all, v_all, low_all, up):
    slots, block, width = k_all.shape
    heads = width // HEAD_SIZE
    rank = up.shape[0]
    group = q.shape[1] // heads
    rows = group // HEAD_SIZE * block
    smem = pl.BlockSpec(memory_space=pltpu.SMEM)
    return pl.pallas_call(
        attention_kernel,
        grid=(heads,),
        in_specs=[
            smem, smem,
            pl.BlockSpec((block, group), lambda k: (0, k)),
            pl.BlockSpec((block, group), lambda k: (0, k)),
            pl.BlockSpec((slots, block, HEAD_SIZE), lambda k: (0, 0, k)),
            pl.BlockSpec((slots, block, HEAD_SIZE), lambda k: (0, 0, k)),
            pl.BlockSpec((slots, rank, block), lambda k: (0, 0, 0)),
            pl.BlockSpec((rank, HEAD_SIZE), lambda k: (0, k)),
        ],
        out_specs=[
            pl.BlockSpec((block, group), lambda k: (0, k)),
            pl.BlockSpec((block, group), lambda k: (0, k)),
            pl.BlockSpec((slots, rank, block), lambda k: (0, 0, 0)),
            pl.BlockSpec((rank, HEAD_SIZE), lambda k: (0, k)),
        ],
        out_shape=[
            jax.ShapeDtypeStruct(q.shape, BF16),
            jax.ShapeDtypeStruct(q.shape, BF16),
            jax.ShapeDtypeStruct((slots, rank, block), F32),
            jax.ShapeDtypeStruct((rank, width), F32),
        ],
        scratch_shapes=[
            pltpu.SMEM((STEPS,), jnp.int32),
            pltpu.VMEM((STEPS, rows, block), F32),
            pltpu.VMEM((rows, HEAD_SIZE), F32),
            pltpu.VMEM((rows, HEAD_SIZE), F32),
            pltpu.VMEM((rows, HEAD_SIZE), BF16),
        ],
        compiler_params=pltpu.CompilerParams(
            dimension_semantics=("arbitrary",), vmem_limit_bytes=48 * 1024 * 1024
        ),
        name="tree_attention",
    )(parents, lengths, q, g, k_all, v_all, low_all, up)


def on_device(x, q, k, frozen, down, up, g, parents, lengths):
    x, q, k, frozen, g = x[0], q[0], k[0], frozen[0], g[0]
    block = x.shape[0]
    slots = lax.axis_size("node")
    low_t = lax.dot_general(
        down, x, (((0,), (1,)), ((), ())), preferred_element_type=F32
    ).astype(BF16)
    values = (frozen.astype(F32) + dot(low_t, up, TN)).astype(BF16)
    k_all = lax.all_gather(k, "node", axis=0)
    v_all = lax.all_gather(values, "node", axis=0)
    low_all = lax.all_gather(low_t, "node", axis=0)
    attended, query_grad, proj, up_sum = attention(
        parents, lengths, q, g, k_all, v_all, low_all, up
    )
    total = lax.psum_scatter(proj, "node", scatter_dimension=0, tiled=True)[0].astype(BF16)
    down_part = dot(total, x, NN)
    down_sum, up_total = lax.psum((down_part, up_sum), ("node", "rep"))
    factor = (slots * lax.axis_size("rep") * block) ** -0.5
    return attended[None], query_grad[None], (down_sum * factor).T, up_total * factor


def solution(mesh):
    rows = P(("groups", "rep"), "node", None)
    table = P(("groups", "rep"), None)
    return jax.shard_map(
        on_device,
        mesh=mesh,
        in_specs=(rows, rows, rows, rows, P(), P(), rows, table, table),
        out_specs=(rows, rows, P("groups", None), P("groups", None)),
        check_vma=False,
    )
```

```python
import functools
import math

import jax
import jax.numpy as jnp
from jax import lax
from jax.experimental import pallas as pl
from jax.experimental.pallas import tpu as pltpu
from jax.sharding import PartitionSpec as P

KEY_HEADS = 4
HEAD_SIZE = 128
PROMPT = 2
SPAN = 5
STEPS = 1 + PROMPT + SPAN
NEGATIVE = -1e30
F32 = jnp.float32
BF16 = jnp.bfloat16
NT = (((1,), (1,)), ((), ()))
NN = (((1,), (0,)), ((), ()))
TN = (((0,), (0,)), ((), ()))


def dot(a, b, dims):
    return lax.dot_general(a, b, dims, preferred_element_type=F32)


def attention_kernel(
    parents, lengths, q_ref, g_ref, own_k, own_v, own_low, k_ref, v_ref, low_ref, up_ref,
    att_ref, qg_ref, proj_ref, upg_ref,
    cand, score, out_acc, qg_acc, grad,
):
    own = lax.axis_index("node")
    head = pl.program_id(0)
    slots, block, _ = k_ref.shape
    per = q_ref.shape[1] // HEAD_SIZE
    rows = per * block
    scale = HEAD_SIZE ** -0.5

    cand[0] = own
    current = own
    count = jnp.int32(1)
    for step in range(1, STEPS):
        parent = parents[0, jnp.maximum(current, 0)]
        current = jnp.where(current >= 0, parent, -1)
        cand[step] = jnp.maximum(current, 0)
        count = count + (current >= 0).astype(jnp.int32)
    own_length = lengths[0, own]

    def stack(ref):
        return jnp.concatenate(
            [ref[:, c * HEAD_SIZE:(c + 1) * HEAD_SIZE] for c in range(per)], axis=0
        )

    live = lax.broadcasted_iota(jnp.int32, (block, HEAD_SIZE), 0) < own_length
    for c in range(per):
        part = g_ref[:, c * HEAD_SIZE:(c + 1) * HEAD_SIZE].astype(F32)
        grad[pl.ds(c * block, block), :] = jnp.where(live, part, 0.0).astype(BF16)
    query = stack(q_ref)

    column = lax.broadcasted_iota(jnp.int32, (block, block), 1)
    row = lax.broadcasted_iota(jnp.int32, (block, block), 0)

    s = dot(query, own_k[...], NT) * (scale * math.log2(math.e))
    allowed = (column <= row) & (column < own_length)
    bias = jnp.where(allowed, 0.0, NEGATIVE)
    bias = jnp.concatenate([bias] * per, axis=0)
    s = jnp.where(bias < 0.0, NEGATIVE, s)
    score[0] = s

    def logits_step(h, top):
        slot = cand[h]
        s = dot(query, k_ref[slot], NT) * (scale * math.log2(math.e))
        col = lax.broadcasted_iota(jnp.int32, (rows, block), 1)
        s = jnp.where(col < lengths[0, slot], s, NEGATIVE)
        score[h] = s
        return jnp.maximum(top, s)

    top = lax.fori_loop(1, count, logits_step, s)
    top = jnp.max(top, axis=1, keepdims=True)

    def exp_step(h, total):
        e = jnp.exp2(score[h] - top)
        score[h] = e
        return total + e

    total = lax.fori_loop(0, count, exp_step, jnp.zeros((rows, block), F32))
    inverse = 1.0 / jnp.sum(total, axis=1, keepdims=True)

    w = score[0] * inverse
    score[0] = w
    out_acc[...] = dot(w.astype(BF16), own_v[...], NN)

    def output_step(h, carry):
        w = score[h] * inverse
        score[h] = w
        out_acc[...] += dot(w.astype(BF16), v_ref[cand[h]], NN)
        return carry

    lax.fori_loop(1, count, output_step, 0)

    dots = jnp.sum(grad[...].astype(F32) * out_acc[...], axis=1, keepdims=True)
    for c in range(per):
        part = out_acc[pl.ds(c * block, block), :]
        att_ref[:, c * HEAD_SIZE:(c + 1) * HEAD_SIZE] = jnp.where(live, part, 0.0).astype(BF16)

    @pl.when(head == 0)
    def _():
        proj_ref[...] = jnp.zeros_like(proj_ref)

    def backward(h, slot, key, value, low):
        g = grad[...]
        w = score[h]
        pressure = dot(g, value, NT)
        slopes = (w * (pressure - dots) * scale).astype(BF16)
        query_part = dot(slopes, key, NN)
        value_grad = dot(w.astype(BF16), g, TN)
        high = value_grad.astype(BF16)
        lowp = (value_grad - high.astype(F32)).astype(BF16)
        proj_ref[slot] += dot(up_ref[...], high, NT) + dot(up_ref[...], lowp, NT)
        return query_part, dot(low, high, NN) + dot(low, lowp, NN)

    qg_acc[...], upg_ref[...] = backward(0, own, own_k[...], own_v[...], own_low[...])

    def backward_step(h, carry):
        slot = cand[h]
        query_part, up_part = backward(h, slot, k_ref[slot], v_ref[slot], low_ref[slot])
        qg_acc[...] += query_part
        upg_ref[...] += up_part
        return carry

    lax.fori_loop(1, count, backward_step, 0)
    for c in range(per):
        qg_ref[:, c * HEAD_SIZE:(c + 1) * HEAD_SIZE] = qg_acc[pl.ds(c * block, block), :].astype(BF16)


def attention(parents, lengths, q, g, k, v, low, k_all, v_all, low_all, up):
    slots, block, width = k_all.shape
    heads = width // HEAD_SIZE
    rank = up.shape[0]
    group = q.shape[1] // heads
    rows = group // HEAD_SIZE * block
    smem = pl.BlockSpec(memory_space=pltpu.SMEM)
    return pl.pallas_call(
        attention_kernel,
        grid=(heads,),
        in_specs=[
            smem, smem,
            pl.BlockSpec((block, group), lambda k: (0, k)),
            pl.BlockSpec((block, group), lambda k: (0, k)),
            pl.BlockSpec((block, HEAD_SIZE), lambda k: (0, k)),
            pl.BlockSpec((block, HEAD_SIZE), lambda k: (0, k)),
            pl.BlockSpec((rank, block), lambda k: (0, 0)),
            pl.BlockSpec((slots, block, HEAD_SIZE), lambda k: (0, 0, k)),
            pl.BlockSpec((slots, block, HEAD_SIZE), lambda k: (0, 0, k)),
            pl.BlockSpec((slots, rank, block), lambda k: (0, 0, 0)),
            pl.BlockSpec((rank, HEAD_SIZE), lambda k: (0, k)),
        ],
        out_specs=[
            pl.BlockSpec((block, group), lambda k: (0, k)),
            pl.BlockSpec((block, group), lambda k: (0, k)),
            pl.BlockSpec((slots, rank, block), lambda k: (0, 0, 0)),
            pl.BlockSpec((rank, HEAD_SIZE), lambda k: (0, k)),
        ],
        out_shape=[
            jax.ShapeDtypeStruct(q.shape, BF16),
            jax.ShapeDtypeStruct(q.shape, BF16),
            jax.ShapeDtypeStruct((slots, rank, block), F32),
            jax.ShapeDtypeStruct((rank, width), F32),
        ],
        scratch_shapes=[
            pltpu.SMEM((STEPS,), jnp.int32),
            pltpu.VMEM((STEPS, rows, block), F32),
            pltpu.VMEM((rows, HEAD_SIZE), F32),
            pltpu.VMEM((rows, HEAD_SIZE), F32),
            pltpu.VMEM((rows, HEAD_SIZE), BF16),
        ],
        compiler_params=pltpu.CompilerParams(
            dimension_semantics=("arbitrary",), vmem_limit_bytes=48 * 1024 * 1024
        ),
        name="tree_attention",
    )(parents, lengths, q, g, k, v, low, k_all, v_all, low_all, up)


def peer(node, rep=None):
    target = {"node": node}
    if rep is not None:
        target["rep"] = rep
    return target


def greet(slots, reps):
    own, rep = lax.axis_index("node"), lax.axis_index("rep")
    barrier = pltpu.get_barrier_semaphore()
    for step in range(reps):
        other = lax.rem(rep + step, lax.axis_size("rep"))

        def signal(t, carry):
            pl.semaphore_signal(
                barrier, inc=1, device_id=peer(lax.rem(own + t, slots), other),
                device_id_type=pl.DeviceIdType.MESH,
            )
            return carry

        lax.fori_loop(0 if step else 1, slots, signal, 0)
    pl.semaphore_wait(barrier, slots * reps - 1)


def reaches(slot, below):
    return (below > slot) & ((slot < PROMPT) | (below - slot <= SPAN))


def share_kernel(slots, *refs):
    own = lax.axis_index("node")
    sources, targets, (send_sem, recv_sem) = refs[:3], refs[3:6], refs[6:]
    greet(slots, 1)

    def copies(local, remote, target):
        return [
            pltpu.make_async_remote_copy(
                src_ref=sources[i], dst_ref=targets[i].at[remote],
                send_sem=send_sem.at[i, target], recv_sem=recv_sem.at[i, remote],
                device_id=peer(target), device_id_type=pl.DeviceIdType.MESH,
            )
            for i in range(3)
        ]

    def start(t, carry):
        @pl.when(reaches(own, t))
        def _():
            for c in copies(own, own, t):
                c.start()
        return carry

    def wait_send(t, carry):
        @pl.when(reaches(own, t))
        def _():
            for c in copies(own, own, t):
                c.wait_send()
        return carry

    def wait_recv(t, carry):
        @pl.when(reaches(t, own))
        def _():
            for c in copies(own, t, t):
                c.wait_recv()
        return carry

    lax.fori_loop(0, slots, start, 0)
    lax.fori_loop(0, slots, wait_recv, 0)
    lax.fori_loop(0, slots, wait_send, 0)


def share(slots, *arrays):
    anywhere = pl.BlockSpec(memory_space=pl.ANY)
    return pl.pallas_call(
        functools.partial(share_kernel, slots),
        in_specs=[anywhere] * 3,
        out_specs=[anywhere] * 3,
        out_shape=[jax.ShapeDtypeStruct((slots, *a.shape), a.dtype) for a in arrays],
        scratch_shapes=[
            pltpu.SemaphoreType.DMA((3, slots)),
            pltpu.SemaphoreType.DMA((3, slots)),
        ],
        compiler_params=pltpu.CompilerParams(collective_id=0, has_side_effects=True),
        name="share_blocks",
    )(*arrays)


def combine_kernel(
    slots, reps, factor, proj, x_ref, upg_ref, down_ref, up_ref,
    landed, total, parts, gathered, result,
    send_p, recv_p, send_r, recv_r, send_g, recv_g,
):
    own, rep = lax.axis_index("node"), lax.axis_index("rep")
    width = x_ref.shape[1]
    up_width = upg_ref.shape[1]
    _, chunks, half, chunk = parts.shape
    mesh_id = pl.DeviceIdType.MESH
    greet(slots, reps)

    def scatter(source, target):
        return pltpu.make_async_remote_copy(
            src_ref=proj.at[target], dst_ref=landed.at[source],
            send_sem=send_p.at[target], recv_sem=recv_p.at[source],
            device_id=peer(target), device_id_type=mesh_id,
        )

    def scatter_start(t, carry):
        @pl.when(reaches(t, own))
        def _():
            scatter(own, t).start()
        return carry

    lax.fori_loop(0, slots, scatter_start, 0)
    total[...] = proj[own]

    def scatter_add(t, carry):
        @pl.when(reaches(own, t))
        def _():
            pltpu.make_async_remote_copy(
                src_ref=proj.at[t], dst_ref=landed.at[t],
                send_sem=send_p.at[t], recv_sem=recv_p.at[t],
                device_id=peer(t), device_id_type=mesh_id,
            ).wait_recv()
            total[...] += landed[t]
        return carry

    lax.fori_loop(0, slots, scatter_add, 0)
    projected = total[...].astype(BF16)
    rank = projected.shape[0]
    for j in range(chunks):
        low, high = j * chunk, (j + 1) * chunk
        pieces = []
        if low < width:
            pieces.append(dot(projected, x_ref[:, low:min(high, width)], NN))
        if high > width and low < width + up_width:
            pieces.append(upg_ref[:, max(low - width, 0):min(high - width, up_width)])
        filled = sum(p.shape[1] for p in pieces)
        if filled < chunk:
            pieces.append(jnp.zeros((rank, chunk - filled), F32))
        value = (pieces[0] if len(pieces) == 1 else jnp.concatenate(pieces, axis=1)).astype(BF16)
        for r in range(reps):
            parts[r, j] = value[r * half:(r + 1) * half]

    def reduce_copy(source, node, r, from_rep):
        return pltpu.make_async_remote_copy(
            src_ref=parts.at[r, node], dst_ref=gathered.at[from_rep, source],
            send_sem=send_r.at[r, node], recv_sem=recv_r.at[from_rep, source],
            device_id=peer(node, r), device_id_type=mesh_id,
        )

    def gather_copy(node, r, owner, owner_rep):
        return pltpu.make_async_remote_copy(
            src_ref=result.at[owner_rep, owner], dst_ref=result.at[owner_rep, owner],
            send_sem=send_g.at[r, node], recv_sem=recv_g.at[owner_rep, owner],
            device_id=peer(node, r), device_id_type=mesh_id,
        )

    def others(action):
        for step in range(reps):
            r = lax.rem(rep + step, reps)

            def body(t, carry):
                action(lax.rem(own + t, slots), r)
                return carry

            lax.fori_loop(0 if step else 1, slots, body, 0)

    def reduce_start(node, r):
        @pl.when(node < chunks)
        def _():
            reduce_copy(own, node, r, rep).start()

    others(reduce_start)

    @pl.when(own < chunks)
    def _():
        gathered[rep, own] = parts[rep, own]

        def reduce_wait(node, r):
            reduce_copy(node, own, rep, r).wait_recv()

        others(reduce_wait)

        def add(t, acc):
            for r in range(reps):
                acc = acc + gathered[r, t].astype(F32)
            return acc

        acc = lax.fori_loop(0, slots, add, jnp.zeros((half, chunk), F32))
        result[rep, own] = (acc * factor).astype(BF16)

        def gather_start(node, r):
            gather_copy(node, r, own, rep).start()

        others(gather_start)

    def gather_wait(node, r):
        @pl.when(node < chunks)
        def _():
            gather_copy(own, rep, node, r).wait_recv()

    others(gather_wait)
    for j in range(chunks):
        low, high = j * chunk, (j + 1) * chunk
        for r in range(reps):
            rows = slice(r * half, (r + 1) * half)
            if low < width:
                end = min(high, width)
                down_ref[rows, low:end] = result[r, j, :, :end - low].astype(F32)
            if high > width and low < width + up_width:
                a, b = max(low, width), min(high, width + up_width)
                up_ref[rows, a - width:b - width] = result[r, j, :, a - low:b - low].astype(F32)

    def scatter_drain(t, carry):
        @pl.when(reaches(t, own))
        def _():
            scatter(own, t).wait_send()
        return carry

    lax.fori_loop(0, slots, scatter_drain, 0)

    def reduce_drain(node, r):
        @pl.when(node < chunks)
        def _():
            reduce_copy(own, node, r, rep).wait_send()

    others(reduce_drain)

    @pl.when(own < chunks)
    def _():
        others(lambda node, r: gather_copy(node, r, own, rep).wait_send())


def combine(slots, reps, factor, proj, x, upg):
    _, rank, block = proj.shape
    width, up_width = x.shape[1], upg.shape[1]
    tiles = -(-(width + up_width) // 128)
    per = -(-tiles // slots)
    chunks = -(-tiles // per)
    chunk = per * 128
    half = rank // reps
    vmem = pl.BlockSpec(memory_space=pltpu.VMEM)
    dma = pltpu.SemaphoreType.DMA
    return pl.pallas_call(
        functools.partial(combine_kernel, slots, reps, factor),
        in_specs=[vmem] * 3,
        out_specs=[vmem] * 2,
        out_shape=[
            jax.ShapeDtypeStruct((rank, width), F32),
            jax.ShapeDtypeStruct((rank, up_width), F32),
        ],
        scratch_shapes=[
            pltpu.VMEM(proj.shape, F32),
            pltpu.VMEM((rank, block), F32),
            pltpu.VMEM((reps, chunks, half, chunk), BF16),
            pltpu.VMEM((reps, slots, half, chunk), BF16),
            pltpu.VMEM((reps, chunks, half, chunk), BF16),
            dma((slots,)), dma((slots,)),
            dma((reps, slots)), dma((reps, slots)),
            dma((reps, slots)), dma((reps, slots)),
        ],
        compiler_params=pltpu.CompilerParams(
            collective_id=1, has_side_effects=True, vmem_limit_bytes=48 * 1024 * 1024
        ),
        name="combine_gradients",
    )(proj, x, upg)


def on_device(x, q, k, frozen, down, up, g, parents, lengths):
    x, q, k, frozen, g = x[0], q[0], k[0], frozen[0], g[0]
    block = x.shape[0]
    slots = lax.axis_size("node")
    low_t = lax.dot_general(
        down, x, (((0,), (1,)), ((), ())), preferred_element_type=F32
    ).astype(BF16)
    values = (frozen.astype(F32) + dot(low_t, up, TN)).astype(BF16)
    k_all, v_all, low_all = share(slots, k, values, low_t)
    attended, query_grad, proj, up_sum = attention(
        parents, lengths, q, g, k, values, low_t, k_all, v_all, low_all, up
    )
    reps = lax.axis_size("rep")
    factor = (slots * reps * block) ** -0.5
    down_sum, up_total = combine(slots, reps, factor, proj, x, up_sum)
    return attended[None], query_grad[None], down_sum.T, up_total


def solution(mesh):
    rows = P(("groups", "rep"), "node", None)
    table = P(("groups", "rep"), None)
    return jax.shard_map(
        on_device,
        mesh=mesh,
        in_specs=(rows, rows, rows, rows, P(), P(), rows, table, table),
        out_specs=(rows, rows, P("groups", None), P("groups", None)),
        check_vma=False,
    )
```

```python
import functools
import math

import jax
import jax.numpy as jnp
from jax import lax
from jax.experimental import pallas as pl
from jax.experimental.pallas import tpu as pltpu
from jax.sharding import PartitionSpec as P

KEY_HEADS = 4
HEAD_SIZE = 128
PROMPT = 2
SPAN = 5
STEPS = 1 + PROMPT + SPAN
NEGATIVE = -1e30
F32 = jnp.float32
BF16 = jnp.bfloat16
NT = (((1,), (1,)), ((), ()))
NN = (((1,), (0,)), ((), ()))
TN = (((0,), (0,)), ((), ()))


def dot(a, b, dims):
    return lax.dot_general(a, b, dims, preferred_element_type=F32)


def attention_kernel(
    parents, lengths, q_ref, g_ref, own_k, own_v, own_low, k_ref, v_ref, low_ref, up_ref,
    att_ref, qg_ref, proj_ref, upg_ref,
    cand, score, out_acc, qg_acc, grad,
):
    own = lax.axis_index("node")
    head = pl.program_id(0)
    slots, block, _ = k_ref.shape
    per = q_ref.shape[1] // HEAD_SIZE
    rows = per * block
    scale = HEAD_SIZE ** -0.5

    cand[0] = own
    current = own
    count = jnp.int32(1)
    for step in range(1, STEPS):
        parent = parents[0, jnp.maximum(current, 0)]
        current = jnp.where(current >= 0, parent, -1)
        cand[step] = jnp.maximum(current, 0)
        count = count + (current >= 0).astype(jnp.int32)
    own_length = lengths[0, own]

    def stack(ref):
        return jnp.concatenate(
            [ref[:, c * HEAD_SIZE:(c + 1) * HEAD_SIZE] for c in range(per)], axis=0
        )

    live = lax.broadcasted_iota(jnp.int32, (block, HEAD_SIZE), 0) < own_length
    for c in range(per):
        part = g_ref[:, c * HEAD_SIZE:(c + 1) * HEAD_SIZE].astype(F32)
        grad[pl.ds(c * block, block), :] = jnp.where(live, part, 0.0).astype(BF16)
    query = stack(q_ref)

    column = lax.broadcasted_iota(jnp.int32, (block, block), 1)
    row = lax.broadcasted_iota(jnp.int32, (block, block), 0)

    s = dot(query, own_k[...], NT) * (scale * math.log2(math.e))
    allowed = (column <= row) & (column < own_length)
    bias = jnp.where(allowed, 0.0, NEGATIVE)
    bias = jnp.concatenate([bias] * per, axis=0)
    s = jnp.where(bias < 0.0, NEGATIVE, s)
    score[0] = s

    def logits_step(h, top):
        slot = cand[h]
        s = dot(query, k_ref[slot], NT) * (scale * math.log2(math.e))
        col = lax.broadcasted_iota(jnp.int32, (rows, block), 1)
        s = jnp.where(col < lengths[0, slot], s, NEGATIVE)
        score[h] = s
        return jnp.maximum(top, s)

    top = lax.fori_loop(1, count, logits_step, s)
    top = jnp.max(top, axis=1, keepdims=True)

    def exp_step(h, total):
        e = jnp.exp2(score[h] - top)
        score[h] = e
        return total + e

    total = lax.fori_loop(0, count, exp_step, jnp.zeros((rows, block), F32))
    inverse = 1.0 / jnp.sum(total, axis=1, keepdims=True)

    w = score[0] * inverse
    score[0] = w
    out_acc[...] = dot(w.astype(BF16), own_v[...], NN)

    def output_step(h, carry):
        w = score[h] * inverse
        score[h] = w
        out_acc[...] += dot(w.astype(BF16), v_ref[cand[h]], NN)
        return carry

    lax.fori_loop(1, count, output_step, 0)

    dots = jnp.sum(grad[...].astype(F32) * out_acc[...], axis=1, keepdims=True)
    for c in range(per):
        part = out_acc[pl.ds(c * block, block), :]
        att_ref[:, c * HEAD_SIZE:(c + 1) * HEAD_SIZE] = jnp.where(live, part, 0.0).astype(BF16)

    @pl.when(head == 0)
    def _():
        proj_ref[...] = jnp.zeros_like(proj_ref)

    def backward(h, slot, key, value, low):
        g = grad[...]
        w = score[h]
        pressure = dot(g, value, NT)
        slopes = (w * (pressure - dots) * scale).astype(BF16)
        query_part = dot(slopes, key, NN)
        value_grad = dot(w.astype(BF16), g, TN)
        high = value_grad.astype(BF16)
        lowp = (value_grad - high.astype(F32)).astype(BF16)
        proj_ref[slot] += dot(up_ref[...], high, NT) + dot(up_ref[...], lowp, NT)
        return query_part, dot(low, high, NN) + dot(low, lowp, NN)

    qg_acc[...], upg_ref[...] = backward(0, own, own_k[...], own_v[...], own_low[...])

    def backward_step(h, carry):
        slot = cand[h]
        query_part, up_part = backward(h, slot, k_ref[slot], v_ref[slot], low_ref[slot])
        qg_acc[...] += query_part
        upg_ref[...] += up_part
        return carry

    lax.fori_loop(1, count, backward_step, 0)
    for c in range(per):
        qg_ref[:, c * HEAD_SIZE:(c + 1) * HEAD_SIZE] = qg_acc[pl.ds(c * block, block), :].astype(BF16)


def attention(parents, lengths, q, g, k, v, low, k_all, v_all, low_all, up):
    slots, block, width = k_all.shape
    heads = width // HEAD_SIZE
    rank = up.shape[0]
    group = q.shape[1] // heads
    rows = group // HEAD_SIZE * block
    smem = pl.BlockSpec(memory_space=pltpu.SMEM)
    return pl.pallas_call(
        attention_kernel,
        grid=(heads,),
        in_specs=[
            smem, smem,
            pl.BlockSpec((block, group), lambda k: (0, k)),
            pl.BlockSpec((block, group), lambda k: (0, k)),
            pl.BlockSpec((block, HEAD_SIZE), lambda k: (0, k)),
            pl.BlockSpec((block, HEAD_SIZE), lambda k: (0, k)),
            pl.BlockSpec((rank, block), lambda k: (0, 0)),
            pl.BlockSpec((slots, block, HEAD_SIZE), lambda k: (0, 0, k)),
            pl.BlockSpec((slots, block, HEAD_SIZE), lambda k: (0, 0, k)),
            pl.BlockSpec((slots, rank, block), lambda k: (0, 0, 0)),
            pl.BlockSpec((rank, HEAD_SIZE), lambda k: (0, k)),
        ],
        out_specs=[
            pl.BlockSpec((block, group), lambda k: (0, k)),
            pl.BlockSpec((block, group), lambda k: (0, k)),
            pl.BlockSpec((slots, rank, block), lambda k: (0, 0, 0)),
            pl.BlockSpec((rank, HEAD_SIZE), lambda k: (0, k)),
        ],
        out_shape=[
            jax.ShapeDtypeStruct(q.shape, BF16),
            jax.ShapeDtypeStruct(q.shape, BF16),
            jax.ShapeDtypeStruct((slots, rank, block), F32),
            jax.ShapeDtypeStruct((rank, width), F32),
        ],
        scratch_shapes=[
            pltpu.SMEM((STEPS,), jnp.int32),
            pltpu.VMEM((STEPS, rows, block), F32),
            pltpu.VMEM((rows, HEAD_SIZE), F32),
            pltpu.VMEM((rows, HEAD_SIZE), F32),
            pltpu.VMEM((rows, HEAD_SIZE), BF16),
        ],
        compiler_params=pltpu.CompilerParams(
            dimension_semantics=("arbitrary",), vmem_limit_bytes=48 * 1024 * 1024
        ),
        name="tree_attention",
    )(parents, lengths, q, g, k, v, low, k_all, v_all, low_all, up)


def peer(node, rep=None):
    target = {"node": node}
    if rep is not None:
        target["rep"] = rep
    return target


def greet(slots, reps):
    own, rep = lax.axis_index("node"), lax.axis_index("rep")
    barrier = pltpu.get_barrier_semaphore()
    for step in range(reps):
        other = lax.rem(rep + step, lax.axis_size("rep"))

        def signal(t, carry):
            pl.semaphore_signal(
                barrier, inc=1, device_id=peer(lax.rem(own + t, slots), other),
                device_id_type=pl.DeviceIdType.MESH,
            )
            return carry

        lax.fori_loop(0 if step else 1, slots, signal, 0)
    pl.semaphore_wait(barrier, slots * reps - 1)


def reaches(slot, below):
    return (below > slot) & ((slot < PROMPT) | (below - slot <= SPAN))


def share_kernel(slots, *refs):
    own = lax.axis_index("node")
    sources, targets, (send_sem, recv_sem) = refs[:3], refs[3:6], refs[6:]
    pair = own // 2
    partner = own + 1 - 2 * lax.rem(own, 2)
    greet(slots, 1)

    def copies(refs, slot, way, target):
        return [
            pltpu.make_async_remote_copy(
                src_ref=refs[i] if refs is sources else refs[i].at[slot],
                dst_ref=targets[i].at[slot],
                send_sem=send_sem.at[way, i, slot], recv_sem=recv_sem.at[i, slot],
                device_id=peer(target), device_id_type=pl.DeviceIdType.MESH,
            )
            for i in range(3)
        ]

    def onward(slot):
        return (own + 2 < slots) & reaches(slot, 2 * pair + 2)

    def each_way(refs, slot, action):
        @pl.when(onward(slot))
        def _():
            for c in copies(refs, slot, 0, own + 2):
                action(c)

        @pl.when(reaches(slot, partner))
        def _():
            for c in copies(refs, slot, 1, partner):
                action(c)

    def relayed(action):
        def body(step, carry):
            slot = own - 2 * step

            @pl.when(reaches(slot, 2 * pair))
            def _():
                action(slot)
            return carry

        lax.fori_loop(1, pair + 1, body, 0)

    def arrived(slot):
        for c in copies(targets, slot, 1, partner):
            c.wait_recv()

    def forward(slot):
        arrived(slot)
        each_way(targets, slot, lambda c: c.start())

    each_way(sources, own, lambda c: c.start())
    relayed(forward)

    def from_partner(step, carry):
        slot = partner - 2 * step

        @pl.when(reaches(slot, own))
        def _():
            arrived(slot)
        return carry

    lax.fori_loop(0, pair + 1, from_partner, 0)
    each_way(sources, own, lambda c: c.wait_send())
    relayed(lambda slot: each_way(targets, slot, lambda c: c.wait_send()))


def share(slots, *arrays):
    anywhere = pl.BlockSpec(memory_space=pl.ANY)
    return pl.pallas_call(
        functools.partial(share_kernel, slots),
        in_specs=[anywhere] * 3,
        out_specs=[anywhere] * 3,
        out_shape=[jax.ShapeDtypeStruct((slots, *a.shape), a.dtype) for a in arrays],
        scratch_shapes=[
            pltpu.SemaphoreType.DMA((2, 3, slots)),
            pltpu.SemaphoreType.DMA((3, slots)),
        ],
        compiler_params=pltpu.CompilerParams(collective_id=0, has_side_effects=True),
        name="share_blocks",
    )(*arrays)


def combine_kernel(
    slots, reps, factor, proj, x_ref, upg_ref, down_ref, up_ref,
    landed, total, parts, gathered, result,
    send_p, recv_p, send_r, recv_r, send_g, recv_g,
):
    own, rep = lax.axis_index("node"), lax.axis_index("rep")
    width = x_ref.shape[1]
    up_width = upg_ref.shape[1]
    _, chunks, half, chunk = parts.shape
    mesh_id = pl.DeviceIdType.MESH
    greet(slots, reps)

    def scatter(source, target):
        return pltpu.make_async_remote_copy(
            src_ref=proj.at[target], dst_ref=landed.at[source],
            send_sem=send_p.at[target], recv_sem=recv_p.at[source],
            device_id=peer(target), device_id_type=mesh_id,
        )

    def scatter_start(t, carry):
        @pl.when(reaches(t, own))
        def _():
            scatter(own, t).start()
        return carry

    lax.fori_loop(0, slots, scatter_start, 0)
    total[...] = proj[own]

    def scatter_add(t, carry):
        @pl.when(reaches(own, t))
        def _():
            pltpu.make_async_remote_copy(
                src_ref=proj.at[t], dst_ref=landed.at[t],
                send_sem=send_p.at[t], recv_sem=recv_p.at[t],
                device_id=peer(t), device_id_type=mesh_id,
            ).wait_recv()
            total[...] += landed[t]
        return carry

    lax.fori_loop(0, slots, scatter_add, 0)
    projected = total[...].astype(BF16)
    rank = projected.shape[0]
    for j in range(chunks):
        low, high = j * chunk, (j + 1) * chunk
        pieces = []
        if low < width:
            pieces.append(dot(projected, x_ref[:, low:min(high, width)], NN))
        if high > width and low < width + up_width:
            pieces.append(upg_ref[:, max(low - width, 0):min(high - width, up_width)])
        filled = sum(p.shape[1] for p in pieces)
        if filled < chunk:
            pieces.append(jnp.zeros((rank, chunk - filled), F32))
        value = (pieces[0] if len(pieces) == 1 else jnp.concatenate(pieces, axis=1)).astype(BF16)
        for r in range(reps):
            parts[r, j] = value[r * half:(r + 1) * half]

    def reduce_copy(source, node, r, from_rep):
        return pltpu.make_async_remote_copy(
            src_ref=parts.at[r, node], dst_ref=gathered.at[from_rep, source],
            send_sem=send_r.at[r, node], recv_sem=recv_r.at[from_rep, source],
            device_id=peer(node, r), device_id_type=mesh_id,
        )

    def gather_copy(node, r, owner, owner_rep):
        return pltpu.make_async_remote_copy(
            src_ref=result.at[owner_rep, owner], dst_ref=result.at[owner_rep, owner],
            send_sem=send_g.at[r, node], recv_sem=recv_g.at[owner_rep, owner],
            device_id=peer(node, r), device_id_type=mesh_id,
        )

    def others(action):
        for step in range(reps):
            r = lax.rem(rep + step, reps)

            def body(t, carry):
                action(lax.rem(own + t, slots), r)
                return carry

            lax.fori_loop(0 if step else 1, slots, body, 0)

    def reduce_start(node, r):
        @pl.when(node < chunks)
        def _():
            reduce_copy(own, node, r, rep).start()

    others(reduce_start)

    @pl.when(own < chunks)
    def _():
        gathered[rep, own] = parts[rep, own]

        def reduce_wait(node, r):
            reduce_copy(node, own, rep, r).wait_recv()

        others(reduce_wait)

        def add(t, acc):
            for r in range(reps):
                acc = acc + gathered[r, t].astype(F32)
            return acc

        acc = lax.fori_loop(0, slots, add, jnp.zeros((half, chunk), F32))
        result[rep, own] = (acc * factor).astype(BF16)

        def gather_start(node, r):
            gather_copy(node, r, own, rep).start()

        others(gather_start)

    def gather_wait(node, r):
        @pl.when(node < chunks)
        def _():
            gather_copy(own, rep, node, r).wait_recv()

    others(gather_wait)
    for j in range(chunks):
        low, high = j * chunk, (j + 1) * chunk
        for r in range(reps):
            rows = slice(r * half, (r + 1) * half)
            if low < width:
                end = min(high, width)
                down_ref[rows, low:end] = result[r, j, :, :end - low].astype(F32)
            if high > width and low < width + up_width:
                a, b = max(low, width), min(high, width + up_width)
                up_ref[rows, a - width:b - width] = result[r, j, :, a - low:b - low].astype(F32)

    def scatter_drain(t, carry):
        @pl.when(reaches(t, own))
        def _():
            scatter(own, t).wait_send()
        return carry

    lax.fori_loop(0, slots, scatter_drain, 0)

    def reduce_drain(node, r):
        @pl.when(node < chunks)
        def _():
            reduce_copy(own, node, r, rep).wait_send()

    others(reduce_drain)

    @pl.when(own < chunks)
    def _():
        others(lambda node, r: gather_copy(node, r, own, rep).wait_send())


def combine(slots, reps, factor, proj, x, upg):
    _, rank, block = proj.shape
    width, up_width = x.shape[1], upg.shape[1]
    tiles = -(-(width + up_width) // 128)
    per = -(-tiles // slots)
    chunks = -(-tiles // per)
    chunk = per * 128
    half = rank // reps
    vmem = pl.BlockSpec(memory_space=pltpu.VMEM)
    dma = pltpu.SemaphoreType.DMA
    return pl.pallas_call(
        functools.partial(combine_kernel, slots, reps, factor),
        in_specs=[vmem] * 3,
        out_specs=[vmem] * 2,
        out_shape=[
            jax.ShapeDtypeStruct((rank, width), F32),
            jax.ShapeDtypeStruct((rank, up_width), F32),
        ],
        scratch_shapes=[
            pltpu.VMEM(proj.shape, F32),
            pltpu.VMEM((rank, block), F32),
            pltpu.VMEM((reps, chunks, half, chunk), BF16),
            pltpu.VMEM((reps, slots, half, chunk), BF16),
            pltpu.VMEM((reps, chunks, half, chunk), BF16),
            dma((slots,)), dma((slots,)),
            dma((reps, slots)), dma((reps, slots)),
            dma((reps, slots)), dma((reps, slots)),
        ],
        compiler_params=pltpu.CompilerParams(
            collective_id=1, has_side_effects=True, vmem_limit_bytes=48 * 1024 * 1024
        ),
        name="combine_gradients",
    )(proj, x, upg)


def on_device(x, q, k, frozen, down, up, g, parents, lengths):
    x, q, k, frozen, g = x[0], q[0], k[0], frozen[0], g[0]
    block = x.shape[0]
    slots = lax.axis_size("node")
    low_t = lax.dot_general(
        down, x, (((0,), (1,)), ((), ())), preferred_element_type=F32
    ).astype(BF16)
    values = (frozen.astype(F32) + dot(low_t, up, TN)).astype(BF16)
    k_all, v_all, low_all = share(slots, k, values, low_t)
    attended, query_grad, proj, up_sum = attention(
        parents, lengths, q, g, k, values, low_t, k_all, v_all, low_all, up
    )
    reps = lax.axis_size("rep")
    factor = (slots * reps * block) ** -0.5
    down_sum, up_total = combine(slots, reps, factor, proj, x, up_sum)
    return attended[None], query_grad[None], down_sum.T, up_total


def solution(mesh):
    rows = P(("groups", "rep"), "node", None)
    table = P(("groups", "rep"), None)
    return jax.shard_map(
        on_device,
        mesh=mesh,
        in_specs=(rows, rows, rows, rows, P(), P(), rows, table, table),
        out_specs=(rows, rows, P("groups", None), P("groups", None)),
        check_vma=False,
    )
```
